256 devices in a mesh: dp: 2 (over x_hi), fsdp: 2 (over core), tensor: 64 (over z, y, x_lo).
Axes of the slice: x: 4 (x_hi: 2, x_lo: 2; x = x_hi * 2 + x_lo), y: 4, z: 8, core: 2. Of those that a mesh axis runs over, the one named last changes fastest.
Arguments:
- weight: float32 [4096, 8192], P('fsdp', 'tensor'), may hold values from -6 to 6
- momentum: float32 [4096, 8192], P('fsdp', 'tensor'), may hold values from -180 to 180
- right_basis: float32 [256, 8192], P('fsdp', 'tensor'), may hold values from -0.0625 to 0.0625
- gradients: bfloat16 [1, 2, 4096, 8192], P(None, 'dp', 'fsdp', 'tensor'), may hold values from -6 to 6
Outputs:
- new_weight: float32 [4096, 8192], P('fsdp', 'tensor')
- new_momentum: float32 [4096, 8192], P('fsdp', 'tensor')
- new_basis: float32 [256, 8192], P('fsdp', 'tensor')
The draws below stay inside these ranges and needn't reach their ends.
All inputs are finite; a program needn't handle non-finite values.
Results may differ from the reference program's by a relative error of at most 0.0003.
Values sent between devices are 32-bit elements; how exact they have to be, the bound alone decides.
No kernel may reach another device: no remote copies, remote signals or barrier semaphores. Data moves between devices by JAX's collectives and lax.ppermute only.
A program may use at most 64 MiB of HBM per device.

```python
import math
import jax
import jax.numpy as jnp
from jax import lax

D = 8192
ROWS = 4096
RANK = 256
STEPS = 1
N_DP = 2


def draw_momentum(key, part):
    base_key, col_key, row_key = jax.random.split(jax.random.fold_in(key, 11), 3)
    column_ramp = jnp.arange(D, dtype=jnp.float32) / D
    col_scale = jnp.exp(math.log(3.0) * column_ramp + jax.random.uniform(col_key, (D,), jnp.float32, 0.0, math.log(10.0)))
    row_scale = jnp.exp(jax.random.uniform(row_key, (ROWS, 1), jnp.float32, 0.0, math.log(4.0)))
    values = jnp.clip(jax.random.normal(base_key, (ROWS, D), jnp.float32), -6.0, 6.0)
    return 0.25 * values * row_scale * col_scale[None, :]


def steps_of(own_key, dims, cuts, least, top_value):
    loudness, own = 1.0, jax.random.fold_in(own_key, 6)
    for position, blocks in cuts:
        heights = jnp.exp(jax.random.uniform(jax.random.fold_in(own, position), (blocks,), jnp.float32, least / len(cuts), top_value / len(cuts)))
        loudness = loudness * jnp.repeat(heights, dims[position] // blocks).reshape([-1 if axis == position else 1 for axis in range(len(dims))])
    return loudness


def normal_values(stream_key, extent, spread, bound, cuts=(), held_as=jnp.bfloat16):
    gain = steps_of(stream_key, extent, cuts, -0.22, 0.18) if cuts else 1.0
    array = jax.random.normal(stream_key, extent, jnp.float32) * spread * gain
    return jnp.minimum(jnp.maximum(array, -bound), bound).astype(held_as)


def setup_inputs(seed: int = 0) -> dict:
    splits = jax.random.split(jax.random.key(seed), 5)
    return {
        "weight": normal_values(splits[0], (ROWS, D), 1.0, 6.0, ((0, 2), (1, 64)), jnp.float32),
        "momentum": draw_momentum(jax.random.fold_in(splits[4], 71), 0),
        "right_basis": normal_values(splits[2], (RANK, D), D ** -0.5, 0.0625, ((0, 2), (1, 64)), jnp.float32),
        "gradients": normal_values(splits[3], (STEPS, N_DP, ROWS, D), 1.0, 6.0, ((1, 2), (2, 2), (3, 64))),
    }


highest = lax.Precision.HIGHEST
step_size = 0.3
drop_share = 0.05
guard_term = 1e-06

def contract(left, right, left_dim, right_dim):
    return lax.dot_general(left.astype(jnp.float32), right.astype(jnp.float32), (((left_dim,), (right_dim,)), ((), ())), precision=highest, preferred_element_type=jnp.float32)

def orthonormal(sketch):
    gram_matrix = contract(sketch, sketch, 0, 0)
    lower_factor = jnp.linalg.cholesky(gram_matrix)
    return lax.linalg.triangular_solve(lower_factor, sketch, left_side=False, lower=True, transpose_a=True)

def reference(weight, momentum, right_basis, gradients):
    step_scale = step_size * math.sqrt(ROWS * D / RANK)
    for iteration in range(STEPS):
        grad_total = gradients[iteration, 0].astype(jnp.float32)
        for replica in range(1, N_DP):
            grad_total = grad_total + gradients[iteration, replica].astype(jnp.float32)
        momentum = momentum + grad_total
        sketch = contract(momentum, right_basis, 1, 1)
        left_basis = orthonormal(sketch)
        coefficients = contract(left_basis, momentum, 0, 0)
        squares = lax.optimization_barrier(jnp.sum(coefficients * coefficients, axis=1))
        right_basis = coefficients * lax.rsqrt(squares + guard_term)[:, None]
        momentum = momentum - drop_share * contract(left_basis, coefficients, 1, 0)
        weight = weight - step_scale * contract(left_basis, right_basis, 1, 0)
    return (weight, momentum, right_basis)
```

```python
import math

import jax
import jax.numpy as jnp
from jax import lax
from jax.experimental import pallas as pl
from jax.experimental.pallas import tpu as pltpu
from jax.sharding import Mesh
from jax.sharding import PartitionSpec as P

D = 8192
ROWS = 4096
RANK = 256


highest = lax.Precision.HIGHEST
step_size = 0.3
drop_share = 0.05
guard_term = 1e-06

PLANE = ("dp", "y", "xl")
TENSOR = ("z", "y", "xl")


def contract(left, right, left_dim, right_dim):
    return lax.dot_general(
        left,
        right,
        (((left_dim,), (right_dim,)), ((), ())),
        precision=highest,
        preferred_element_type=jnp.float32,
    )


def swapped(value, axis):
    return lax.ppermute(value, axis, [(0, 1), (1, 0)])


def sent_to_all(value, axis):
    length = lax.axis_size(axis)
    return lax.all_to_all(
        jnp.broadcast_to(value[None], (length, *value.shape)), axis, 0, 0, tiled=True
    )


def sum_at_owner(value, axis):
    length = lax.axis_size(axis)
    pieces = value.reshape(length, len(value) // length, *value.shape[1:])
    return lax.all_to_all(pieces, axis, 0, 0, tiled=True).sum(axis=0)


def gather(value, axis):
    pieces = sent_to_all(value, axis)
    return pieces.reshape(-1, *value.shape[1:])


BLOCK = 64
TILE = 8


def block_inverse(block):
    size = len(block)
    rows = lax.broadcasted_iota(jnp.int32, (size, size), 0)
    columns = lax.broadcasted_iota(jnp.int32, (size, size), 1)
    identity = (rows == columns).astype(jnp.float32)
    both = jnp.concatenate([block, identity], axis=1)
    tiles = [both[TILE * t : TILE * t + TILE] for t in range(size // TILE)]
    in_tile = lax.broadcasted_iota(jnp.int32, (TILE, 1), 0)
    for k in range(size - 1):
        t, s = divmod(k, TILE)
        row = tiles[t][s : s + 1]
        scaled = row * (1.0 / row[:, k : k + 1])
        for u in range(t, size // TILE):
            column = tiles[u][:, k : k + 1]
            if u == t:
                if s == TILE - 1:
                    continue
                column = jnp.where(in_tile > s, column, 0.0)
            tiles[u] = tiles[u] - column * scaled
    both = jnp.concatenate(tiles, axis=0)
    pivots = jnp.sum(jnp.where(rows == columns, both[:, :size], 0.0), axis=1, keepdims=True)
    return both[:, size:] * lax.rsqrt(pivots)


def inverse_factor_kernel(own_ref, other_ref, out_ref, held):
    held[...] = own_ref[...] + other_ref[...]
    for first in range(0, RANK, BLOCK):
        last = first + BLOCK
        inverse = block_inverse(held[first:last, first:last])
        lane = lax.broadcasted_iota(jnp.int32, (BLOCK, RANK), 1)
        row = lax.broadcasted_iota(jnp.int32, (BLOCK, RANK), 0)
        inside = (lane >= first) & (lane < last)
        panel = jnp.where(inside, (lane - first == row).astype(jnp.float32), held[first:last, :])
        panel = contract(inverse, panel, 1, 0)
        held[first:last, :] = panel
        if last < RANK:
            rest = held[last:, :]
            factor = contract(rest[:, first:last], inverse, 1, 1)
            lane = lax.broadcasted_iota(jnp.int32, (RANK - last, RANK), 1)
            inside = (lane >= first) & (lane < last)
            held[last:, :] = jnp.where(inside, 0.0, rest) - contract(factor, panel, 1, 0)
    row = lax.broadcasted_iota(jnp.int32, (RANK, RANK), 0)
    lane = lax.broadcasted_iota(jnp.int32, (RANK, RANK), 1)
    out_ref[...] = jnp.where(lane <= row, held[...], 0.0)


def inverse_factor(own, other):
    return pl.pallas_call(
        inverse_factor_kernel,
        out_shape=jax.ShapeDtypeStruct((RANK, RANK), jnp.float32),
        in_specs=[pl.BlockSpec(memory_space=pltpu.VMEM)] * 2,
        out_specs=pl.BlockSpec(memory_space=pltpu.VMEM),
        scratch_shapes=[pltpu.VMEM((RANK, RANK), jnp.float32)],
        cost_estimate=pl.CostEstimate(
            flops=60_000_000_000, bytes_accessed=3 * 4 * RANK * RANK, transcendentals=0
        ),
    )(own, other)


def shards(weight, momentum, right_basis, gradients):
    step_scale = step_size * math.sqrt(ROWS * D / RANK)
    share = len(right_basis)
    second = lax.axis_index("fsdp") == 1
    gradient = gradients[0, 0].astype(jnp.float32)
    other_basis = swapped(right_basis, "fsdp")
    basis = jnp.concatenate(
        [
            jnp.where(second, other_basis, right_basis),
            jnp.where(second, right_basis, other_basis),
        ],
        axis=0,
    )
    part = 0.5 * momentum + gradient
    sketch = sum_at_owner(contract(part, basis, 1, 1), PLANE)
    sketch = sum_at_owner(sketch, "z")
    sketch = gather(gather(sketch, "z"), PLANE)

    gram = contract(sketch, sketch, 0, 0)
    product = contract(sketch, part, 0, 0)
    other_gram = swapped(gram, "fsdp")
    product = product + swapped(product, "fsdp")
    product = product + swapped(product, "dp")
    held_gradient, _ = lax.optimization_barrier((gradient, gram))
    other_gradient = swapped(held_gradient, "dp")

    inverse = inverse_factor(gram, other_gram)
    coefficients = contract(inverse, product, 1, 0)
    squares = sent_to_all(jnp.sum(coefficients * coefficients, axis=1)[None], TENSOR)
    scale = lax.rsqrt(jnp.sum(squares, axis=(0, 1)) + guard_term)
    new_basis = coefficients * scale[:, None]
    momentum = momentum + (gradient + other_gradient)
    momentum = momentum - drop_share * contract(sketch, contract(inverse, coefficients, 0, 0), 1, 0)
    weight = weight - step_scale * contract(sketch, contract(inverse, new_basis, 0, 0), 1, 0)
    first = lax.axis_index("fsdp") * share
    return weight, momentum, lax.dynamic_slice_in_dim(new_basis, first, share, 0)


def solution(mesh):
    fine = Mesh(mesh.devices.reshape(2, 2, 8, 4, 2), ("dp", "fsdp", "z", "y", "xl"))
    placed = P("fsdp", TENSOR)
    return jax.shard_map(
        shards,
        mesh=fine,
        in_specs=(placed, placed, placed, P(None, "dp", "fsdp", TENSOR)),
        out_specs=(placed, placed, placed),
        check_vma=False,
    )
```

```python
import math

import jax
import jax.numpy as jnp
from jax import lax
from jax.experimental import pallas as pl
from jax.experimental.pallas import tpu as pltpu
from jax.sharding import Mesh
from jax.sharding import PartitionSpec as P

D = 8192
ROWS = 4096
RANK = 256


highest = lax.Precision.HIGHEST
step_size = 0.3
drop_share = 0.05
guard_term = 1e-06

PLANE = ("dp", "y", "xl")
TENSOR = ("z", "y", "xl")


def contract(left, right, left_dim, right_dim):
    return lax.dot_general(
        left,
        right,
        (((left_dim,), (right_dim,)), ((), ())),
        precision=highest,
        preferred_element_type=jnp.float32,
    )


def in_hbm(value):
    return pltpu.with_memory_space_constraint(value, pltpu.HBM)


def swapped(value, axis):
    return lax.ppermute(value, axis, [(0, 1), (1, 0)])


def sent_to_all(value, axis):
    length = lax.axis_size(axis)
    return lax.all_to_all(
        jnp.broadcast_to(value[None], (length, *value.shape)), axis, 0, 0, tiled=True
    )


def sum_at_owner(value, axis):
    length = lax.axis_size(axis)
    pieces = value.reshape(length, len(value) // length, *value.shape[1:])
    return lax.all_to_all(pieces, axis, 0, 0, tiled=True).sum(axis=0)


def gather(value, axis):
    pieces = sent_to_all(value, axis)
    return pieces.reshape(-1, *value.shape[1:])


KERNEL_VMEM = 16 * 2**20
BLOCK = 64
TILE = 8


def block_inverse(block):
    size = len(block)
    rows = lax.broadcasted_iota(jnp.int32, (size, size), 0)
    columns = lax.broadcasted_iota(jnp.int32, (size, size), 1)
    identity = (rows == columns).astype(jnp.float32)
    both = jnp.concatenate([block, identity], axis=1)
    tiles = [both[TILE * t : TILE * t + TILE] for t in range(size // TILE)]
    in_tile = lax.broadcasted_iota(jnp.int32, (TILE, 1), 0)
    for k in range(size - 1):
        t, s = divmod(k, TILE)
        row = tiles[t][s : s + 1]
        scaled = row * (1.0 / row[:, k : k + 1])
        for u in range(t, size // TILE):
            column = tiles[u][:, k : k + 1]
            if u == t:
                if s == TILE - 1:
                    continue
                column = jnp.where(in_tile > s, column, 0.0)
            tiles[u] = tiles[u] - column * scaled
    both = jnp.concatenate(tiles, axis=0)
    pivots = jnp.sum(jnp.where(rows == columns, both[:, :size], 0.0), axis=1, keepdims=True)
    return both[:, size:] * lax.rsqrt(pivots)


def split(value):
    high = value.astype(jnp.bfloat16)
    return high, (value - high.astype(jnp.float32)).astype(jnp.bfloat16)


def three_pass(left, right, left_dim, right_dim):
    def product(a, b):
        return lax.dot_general(
            a, b, (((left_dim,), (right_dim,)), ((), ())), preferred_element_type=jnp.float32
        )

    left_high, left_low = split(left)
    right_high, right_low = split(right)
    return product(left_high, right_high) + (
        product(left_high, right_low) + product(left_low, right_high)
    )


def moments_kernel(sketch_ref, momentum_ref, own_ref, other_ref, gram_ref, product_ref, total_ref):
    @pl.when(pl.program_id(0) == 0)
    def _():
        gram_ref[...] = jnp.zeros_like(gram_ref)
        product_ref[...] = jnp.zeros_like(product_ref)

    sketch = sketch_ref[...]
    total = momentum_ref[...] + (own_ref[...].astype(jnp.float32) + other_ref[...])
    total_ref[...] = total
    gram_ref[...] += contract(sketch, sketch, 0, 0)
    product_ref[...] += three_pass(sketch, total, 0, 0)


def moments(sketch, momentum, own, other):
    rows, columns = momentum.shape
    step = rows // 4

    def by_rows(width):
        return pl.BlockSpec((step, width), lambda i: (i, 0))

    def whole(*shape):
        return pl.BlockSpec(shape, lambda i: (0, 0))

    return pl.pallas_call(
        moments_kernel,
        compiler_params=pltpu.CompilerParams(vmem_limit_bytes=KERNEL_VMEM),
        grid=(rows // step,),
        out_shape=(
            jax.ShapeDtypeStruct((RANK, RANK), jnp.float32),
            jax.ShapeDtypeStruct((RANK, columns), jnp.float32),
            pltpu.HBM((rows, columns), jnp.float32),
        ),
        in_specs=[by_rows(RANK), by_rows(columns), by_rows(columns), by_rows(columns)],
        out_specs=(whole(RANK, RANK), whole(RANK, columns), by_rows(columns)),
    )(sketch, in_hbm(momentum), in_hbm(own), other)


def coefficients_kernel(
    gram_ref, other_gram_ref, product_ref, other_product_ref,
    inverse_ref, coefficients_ref, squares_ref, held,
):
    held[...] = gram_ref[...] + other_gram_ref[...]
    for first in range(0, RANK, BLOCK):
        last = first + BLOCK
        inverse = block_inverse(held[first:last, first:last])
        lane = lax.broadcasted_iota(jnp.int32, (BLOCK, RANK), 1)
        row = lax.broadcasted_iota(jnp.int32, (BLOCK, RANK), 0)
        inside = (lane >= first) & (lane < last)
        panel = jnp.where(inside, (lane - first == row).astype(jnp.float32), held[first:last, :])
        panel = contract(inverse, panel, 1, 0)
        held[first:last, :] = panel
        if last < RANK:
            rest = held[last:, :]
            factor = contract(rest[:, first:last], inverse, 1, 1)
            lane = lax.broadcasted_iota(jnp.int32, (RANK - last, RANK), 1)
            inside = (lane >= first) & (lane < last)
            held[last:, :] = jnp.where(inside, 0.0, rest) - contract(factor, panel, 1, 0)
    row = lax.broadcasted_iota(jnp.int32, (RANK, RANK), 0)
    lane = lax.broadcasted_iota(jnp.int32, (RANK, RANK), 1)
    inverse = jnp.where(lane <= row, held[...], 0.0)
    coefficients = contract(inverse, product_ref[...] + other_product_ref[...], 1, 0)
    coefficients_ref[...] = coefficients
    inverse_ref[...] = inverse.T
    ones = jnp.ones((8, coefficients.shape[1]), jnp.float32)
    squares = contract(ones, coefficients * coefficients, 1, 1)
    squares_ref[...] = jnp.broadcast_to(squares[None, :1], squares_ref.shape)


def small_part(gram, other_gram, product, other_product, copies):
    def whole(shape):
        return pl.BlockSpec(shape, lambda i: (0,) * len(shape))

    return pl.pallas_call(
        coefficients_kernel,
        compiler_params=pltpu.CompilerParams(vmem_limit_bytes=KERNEL_VMEM),
        out_shape=(
            pltpu.HBM(gram.shape, jnp.float32),
            pltpu.HBM(product.shape, jnp.float32),
            jax.ShapeDtypeStruct((copies, 1, RANK), jnp.float32),
        ),
        in_specs=[pl.BlockSpec(memory_space=pltpu.VMEM)] * 4,
        grid=(1,),
        out_specs=(whole(gram.shape), whole(product.shape), whole((copies, 1, RANK))),
        scratch_shapes=[pltpu.VMEM((RANK, RANK), jnp.float32)],
    )(gram, other_gram, product, other_product)


def update_kernel(
    first_ref, squares_ref, sketch_ref, inverse_ref, coefficients_ref, weight_ref, total_ref,
    weight_out_ref, momentum_out_ref, basis_ref, change_ref,
):
    columns = weight_ref.shape[1]

    @pl.when(pl.program_id(0) == 0)
    def _():
        step_scale = step_size * math.sqrt(ROWS * D / RANK)
        scale = lax.rsqrt(jnp.sum(squares_ref[:, 0, :], axis=0, keepdims=True) + guard_term)
        inverse = inverse_ref[...]
        coefficients = coefficients_ref[...]
        change_ref[:, :columns] = step_scale * contract(inverse * scale, coefficients, 1, 0)
        change_ref[:, columns:] = drop_share * contract(inverse, coefficients, 1, 0)
        share = basis_ref.shape[0]
        row = lax.broadcasted_iota(jnp.int32, (share, RANK), 0) + first_ref[0]
        lane = lax.broadcasted_iota(jnp.int32, (share, RANK), 1)
        column = jnp.sum(jnp.where(row == lane, scale, 0.0), axis=1, keepdims=True)
        first = pl.multiple_of(first_ref[0], share)
        basis_ref[...] = coefficients_ref[pl.ds(first, share), :] * column

    change = three_pass(sketch_ref[...], change_ref[...], 1, 0)
    weight_out_ref[...] = weight_ref[...] - change[:, :columns]
    momentum_out_ref[...] = total_ref[...] - change[:, columns:]


def updates(first, squares, sketch, inverse, coefficients, weight, total, share):
    rows, columns = weight.shape
    step = rows // 4

    def whole(array):
        return pl.BlockSpec(array.shape, lambda i, first: (0,) * array.ndim)

    def by_rows(width):
        return pl.BlockSpec((step, width), lambda i, first: (i, 0))

    return pl.pallas_call(
        update_kernel,
        compiler_params=pltpu.CompilerParams(vmem_limit_bytes=KERNEL_VMEM),
        grid_spec=pltpu.PrefetchScalarGridSpec(
            num_scalar_prefetch=1,
            grid=(rows // step,),
            in_specs=[
                whole(squares),
                by_rows(RANK),
                whole(inverse),
                whole(coefficients),
                by_rows(columns),
                by_rows(columns),
            ],
            out_specs=(
                by_rows(columns),
                by_rows(columns),
                pl.BlockSpec((share, columns), lambda i, first: (0, 0)),
            ),
            scratch_shapes=[pltpu.VMEM((RANK, 2 * columns), jnp.float32)],
        ),
        out_shape=(
            jax.ShapeDtypeStruct(weight.shape, jnp.float32),
            jax.ShapeDtypeStruct(weight.shape, jnp.float32),
            jax.ShapeDtypeStruct((share, columns), jnp.float32),
        ),
    )(
        first, squares, sketch, in_hbm(inverse), in_hbm(coefficients), in_hbm(weight), in_hbm(total)
    )


def split_in_three(value):
    high, _ = split(value)
    middle = value - high.astype(jnp.float32)
    middle_part = middle.astype(jnp.bfloat16)
    return high, middle_part, (middle - middle_part.astype(jnp.float32)).astype(jnp.bfloat16)


def term_kernel(core_ref, momentum_ref, gradient_ref, own_ref, other_ref, term_ref, wide_ref):
    gradient = gradient_ref[...].astype(jnp.float32)
    wide_ref[...] = gradient
    a1, a2, a3 = split_in_three(0.5 * momentum_ref[...] + gradient)
    left, right = jnp.concatenate([a1, a2], axis=1), jnp.concatenate([a1, a3], axis=1)

    def product(a, b):
        return lax.dot_general(
            a, b, (((1,), (1,)), ((), ())), preferred_element_type=jnp.float32
        )

    halves = []
    for half in range(2):
        basis = jnp.where(core_ref[0] == half, own_ref[...], other_ref[...])
        b1, b2, b3 = split_in_three(basis)
        halves.append(
            product(left, jnp.concatenate([b1, b1], axis=1))
            + (
                product(left, jnp.concatenate([b2, b2], axis=1))
                + product(right, jnp.concatenate([b3, b1], axis=1))
            )
        )
    term_ref[...] = jnp.concatenate(halves, axis=1)


def sketch_term(core, momentum, gradient, own, other):
    rows, columns = momentum.shape
    step = rows // 4

    def by_rows(width):
        return pl.BlockSpec((step, width), lambda i, core: (i, 0))

    def whole(array):
        return pl.BlockSpec(array.shape, lambda i, core: (0, 0))

    return pl.pallas_call(
        term_kernel,
        compiler_params=pltpu.CompilerParams(vmem_limit_bytes=KERNEL_VMEM),
        grid_spec=pltpu.PrefetchScalarGridSpec(
            num_scalar_prefetch=1,
            grid=(rows // step,),
            in_specs=[by_rows(columns), by_rows(columns), whole(own), whole(other)],
            out_specs=(by_rows(RANK), by_rows(columns)),
        ),
        out_shape=(
            jax.ShapeDtypeStruct((rows, RANK), jnp.float32),
            jax.ShapeDtypeStruct((rows, columns), jnp.float32),
        ),
    )(core, in_hbm(momentum), in_hbm(gradient), in_hbm(own), other)


def step(weight, momentum, right_basis, gradients):
    share = len(right_basis)
    core = jnp.reshape(lax.axis_index("fsdp"), (1,)).astype(jnp.int32)
    own = gradients[0, 0]
    term, gradient = sketch_term(core, momentum, own, right_basis, swapped(right_basis, "fsdp"))
    sketch = sum_at_owner(term, PLANE)
    gradient, sketch = lax.optimization_barrier((gradient, sketch))
    other = swapped(gradient, "dp")
    sketch = sum_at_owner(sketch, "z")
    sketch = gather(sketch, "z")
    other, sketch = lax.optimization_barrier((other, sketch))
    sketch = gather(sketch, PLANE)

    gram, product, total = moments(sketch, momentum, own, other)
    inverse, coefficients, squares = small_part(
        gram, swapped(gram, "fsdp"), product, swapped(product, "fsdp"), lax.axis_size(TENSOR)
    )
    squares = lax.all_to_all(squares, TENSOR, 0, 0, tiled=True)
    weight, momentum, right_basis = updates(
        core * share, squares, sketch, inverse, coefficients, weight, total, share
    )
    return weight, momentum, right_basis


def solution(mesh):
    fine = Mesh(mesh.devices.reshape(2, 2, 8, 4, 2), ("dp", "fsdp", "z", "y", "xl"))
    placed = P("fsdp", TENSOR)
    return jax.shard_map(
        step,
        mesh=fine,
        in_specs=(placed, placed, placed, P(None, "dp", "fsdp", TENSOR)),
        out_specs=(placed, placed, placed),
        check_vma=False,
    )
```

```python
import math

import jax
import jax.numpy as jnp
from jax import lax
from jax.experimental import pallas as pl
from jax.experimental.pallas import tpu as pltpu
from jax.sharding import Mesh
from jax.sharding import PartitionSpec as P

D = 8192
ROWS = 4096
RANK = 256


highest = lax.Precision.HIGHEST
step_size = 0.3
drop_share = 0.05
guard_term = 1e-06

NEAR = ("dp", "zl", "y", "xl")
TENSOR = ("zh", "zl", "y", "xl")


def contract(left, right, left_dim, right_dim):
    return lax.dot_general(
        left,
        right,
        (((left_dim,), (right_dim,)), ((), ())),
        precision=highest,
        preferred_element_type=jnp.float32,
    )


def in_hbm(value):
    return pltpu.with_memory_space_constraint(value, pltpu.HBM)


def swapped(value, axis):
    return lax.ppermute(value, axis, [(0, 1), (1, 0)])


def sent_to_all(value, axis):
    length = lax.axis_size(axis)
    return lax.all_to_all(
        jnp.broadcast_to(value[None], (length, *value.shape)), axis, 0, 0, tiled=True
    )


def sum_at_owner(value, axis):
    length = lax.axis_size(axis)
    pieces = value.reshape(length, len(value) // length, *value.shape[1:])
    return lax.all_to_all(pieces, axis, 0, 0, tiled=True).sum(axis=0)


def gather(value, axis):
    pieces = sent_to_all(value, axis)
    return pieces.reshape(-1, *value.shape[1:])


KERNEL_VMEM = 16 * 2**20
BLOCK = 64
TILE = 8


def block_inverse(block):
    size = len(block)
    width = 2 * size
    rows = lax.broadcasted_iota(jnp.int32, (size, size), 0)
    columns = lax.broadcasted_iota(jnp.int32, (size, size), 1)
    both = jnp.concatenate([block, (rows == columns).astype(jnp.float32)], axis=1)
    tiles = [both[first : first + TILE] for first in range(0, size, TILE)]
    place = lax.broadcasted_iota(jnp.int32, (TILE, width), 0)

    def column(value, k):
        return jnp.broadcast_to(value[:, k : k + 1], (TILE, width))

    def row(value, k):
        return jnp.broadcast_to(value[k : k + 1, :], (TILE, width))

    def stacked(values):
        result = values[0]
        for k in range(1, TILE):
            result = jnp.where(place == k, values[k], result)
        return result

    finished = []
    for t, tile in enumerate(tiles):
        entry, factor, reciprocal, inverse = {}, {}, {}, {}
        for j in range(TILE):
            spread = column(tile, TILE * t + j)
            for i in range(j, TILE):
                entry[i, j] = row(spread, i)
        for j in range(TILE):
            reciprocal[j] = 1.0 / entry[j, j]
            for i in range(j + 1, TILE):
                factor[i, j] = entry[i, j] * reciprocal[j]
                for k in range(j + 1, i + 1):
                    entry[i, k] = entry[i, k] - factor[i, j] * entry[k, j]
        for j in range(TILE):
            for i in range(j + 1, TILE):
                total = factor[i, j]
                for k in range(j + 1, i):
                    total = total + factor[i, k] * inverse[k, j]
                inverse[i, j] = -total
        old = [row(tile, i) for i in range(TILE)]
        new = []
        for i in range(TILE):
            total = old[i]
            for j in range(i):
                total = total + inverse[i, j] * old[j]
            new.append(total)
        finished.append(stacked(new) * lax.rsqrt(stacked([entry[j, j] for j in range(TILE)])))
        for u in range(t + 1, size // TILE):
            spread = [column(tiles[u], TILE * t + j) for j in range(TILE)]
            rest = tiles[u]
            for j in range(TILE):
                total = spread[j]
                for k in range(j):
                    total = total + inverse[j, k] * spread[k]
                rest = rest - (total * reciprocal[j]) * new[j]
            tiles[u] = rest
    return jnp.concatenate(finished, axis=0)[:, size:]


def split(value):
    high = value.astype(jnp.bfloat16)
    return high, (value - high.astype(jnp.float32)).astype(jnp.bfloat16)


def three_pass(left, right, left_dim, right_dim):
    def product(a, b):
        return lax.dot_general(
            a, b, (((left_dim,), (right_dim,)), ((), ())), preferred_element_type=jnp.float32
        )

    left_high, left_low = split(left)
    right_high, right_low = split(right)
    return product(left_high, right_high) + (
        product(left_high, right_low) + product(left_low, right_high)
    )


def moments_kernel(
    replica_ref, sketch_ref, momentum_ref, own_ref, near_ref, far_ref,
    gram_ref, product_ref, total_ref,
):
    step = pl.program_id(0)

    @pl.when(step == 0)
    def _():
        gram_ref[...] = jnp.zeros_like(gram_ref)
        product_ref[...] = jnp.zeros_like(product_ref)

    sketch = sketch_ref[...]
    in_own_half = step // (pl.num_programs(0) // 2) == replica_ref[0]
    other = jnp.where(in_own_half, near_ref[...], far_ref[...])
    total = momentum_ref[...] + (own_ref[...].astype(jnp.float32) + other)
    total_ref[...] = total
    gram_ref[...] += contract(sketch, sketch, 0, 0)
    product_ref[...] += three_pass(sketch, total, 0, 0)


def moments(replica, sketch, momentum, own, near, far):
    rows, columns = momentum.shape
    steps = 4
    step = rows // steps

    def by_rows(width):
        return pl.BlockSpec((step, width), lambda i, replica: (i, 0))

    def by_half(width):
        return pl.BlockSpec((step, width), lambda i, replica: (i % (steps // 2), 0))

    def whole(*shape):
        return pl.BlockSpec(shape, lambda i, replica: (0, 0))

    return pl.pallas_call(
        moments_kernel,
        compiler_params=pltpu.CompilerParams(vmem_limit_bytes=KERNEL_VMEM),
        grid_spec=pltpu.PrefetchScalarGridSpec(
            num_scalar_prefetch=1,
            grid=(steps,),
            in_specs=[
                by_rows(RANK),
                by_rows(columns),
                by_rows(columns),
                by_half(columns),
                by_half(columns),
            ],
            out_specs=(whole(RANK, RANK), whole(RANK, columns), by_rows(columns)),
        ),
        out_shape=(
            jax.ShapeDtypeStruct((RANK, RANK), jnp.float32),
            jax.ShapeDtypeStruct((RANK, columns), jnp.float32),
            pltpu.HBM((rows, columns), jnp.float32),
        ),
    )(replica, sketch, in_hbm(momentum), in_hbm(own), near, far)


def coefficients_kernel(
    gram_ref, other_gram_ref, product_ref, other_product_ref,
    inverse_ref, coefficients_ref, squares_ref, held,
):
    held[...] = gram_ref[...] + other_gram_ref[...]
    for first in range(0, RANK, BLOCK):
        last = first + BLOCK
        inverse = block_inverse(held[first:last, first:last])
        lane = lax.broadcasted_iota(jnp.int32, (BLOCK, RANK), 1)
        row = lax.broadcasted_iota(jnp.int32, (BLOCK, RANK), 0)
        inside = (lane >= first) & (lane < last)
        panel = jnp.where(inside, (lane - first == row).astype(jnp.float32), held[first:last, :])
        panel = contract(inverse, panel, 1, 0)
        held[first:last, :] = panel
        if last < RANK:
            rest = held[last:, :]
            factor = contract(rest[:, first:last], inverse, 1, 1)
            lane = lax.broadcasted_iota(jnp.int32, (RANK - last, RANK), 1)
            inside = (lane >= first) & (lane < last)
            held[last:, :] = jnp.where(inside, 0.0, rest) - contract(factor, panel, 1, 0)
    row = lax.broadcasted_iota(jnp.int32, (RANK, RANK), 0)
    lane = lax.broadcasted_iota(jnp.int32, (RANK, RANK), 1)
    inverse = jnp.where(lane <= row, held[...], 0.0)
    coefficients = contract(inverse, product_ref[...] + other_product_ref[...], 1, 0)
    coefficients_ref[...] = coefficients
    inverse_ref[...] = inverse.T
    ones = jnp.ones((8, coefficients.shape[1]), jnp.float32)
    squares = contract(ones, coefficients * coefficients, 1, 1)
    squares_ref[...] = jnp.broadcast_to(squares[None, :1], squares_ref.shape)


def small_part(gram, other_gram, product, other_product, copies):
    def whole(shape):
        return pl.BlockSpec(shape, lambda i: (0,) * len(shape))

    return pl.pallas_call(
        coefficients_kernel,
        compiler_params=pltpu.CompilerParams(vmem_limit_bytes=KERNEL_VMEM),
        out_shape=(
            pltpu.HBM(gram.shape, jnp.float32),
            pltpu.HBM(product.shape, jnp.float32),
            jax.ShapeDtypeStruct((copies, 1, RANK), jnp.float32),
        ),
        in_specs=[pl.BlockSpec(memory_space=pltpu.VMEM)] * 4,
        grid=(1,),
        out_specs=(whole(gram.shape), whole(product.shape), whole((copies, 1, RANK))),
        scratch_shapes=[pltpu.VMEM((RANK, RANK), jnp.float32)],
    )(gram, other_gram, product, other_product)


def update_kernel(
    first_ref, squares_ref, sketch_ref, inverse_ref, coefficients_ref, weight_ref, total_ref,
    weight_out_ref, momentum_out_ref, basis_ref, change_ref,
):
    columns = weight_ref.shape[1]

    @pl.when(pl.program_id(0) == 0)
    def _():
        step_scale = step_size * math.sqrt(ROWS * D / RANK)
        scale = lax.rsqrt(jnp.sum(squares_ref[:, 0, :], axis=0, keepdims=True) + guard_term)
        inverse = inverse_ref[...]
        coefficients = coefficients_ref[...]
        change_ref[:, :columns] = step_scale * contract(inverse * scale, coefficients, 1, 0)
        change_ref[:, columns:] = drop_share * contract(inverse, coefficients, 1, 0)
        share = basis_ref.shape[0]
        row = lax.broadcasted_iota(jnp.int32, (share, RANK), 0) + first_ref[0]
        lane = lax.broadcasted_iota(jnp.int32, (share, RANK), 1)
        column = jnp.sum(jnp.where(row == lane, scale, 0.0), axis=1, keepdims=True)
        first = pl.multiple_of(first_ref[0], share)
        basis_ref[...] = coefficients_ref[pl.ds(first, share), :] * column

    change = three_pass(sketch_ref[...], change_ref[...], 1, 0)
    weight_out_ref[...] = weight_ref[...] - change[:, :columns]
    momentum_out_ref[...] = total_ref[...] - change[:, columns:]


def updates(first, squares, sketch, inverse, coefficients, weight, total, share):
    rows, columns = weight.shape
    step = rows // 4

    def whole(array):
        return pl.BlockSpec(array.shape, lambda i, first: (0,) * array.ndim)

    def by_rows(width):
        return pl.BlockSpec((step, width), lambda i, first: (i, 0))

    return pl.pallas_call(
        update_kernel,
        compiler_params=pltpu.CompilerParams(vmem_limit_bytes=KERNEL_VMEM),
        grid_spec=pltpu.PrefetchScalarGridSpec(
            num_scalar_prefetch=1,
            grid=(rows // step,),
            in_specs=[
                whole(squares),
                by_rows(RANK),
                whole(inverse),
                whole(coefficients),
                by_rows(columns),
                by_rows(columns),
            ],
            out_specs=(
                by_rows(columns),
                by_rows(columns),
                pl.BlockSpec((share, columns), lambda i, first: (0, 0)),
            ),
            scratch_shapes=[pltpu.VMEM((RANK, 2 * columns), jnp.float32)],
        ),
        out_shape=(
            jax.ShapeDtypeStruct(weight.shape, jnp.float32),
            jax.ShapeDtypeStruct(weight.shape, jnp.float32),
            jax.ShapeDtypeStruct((share, columns), jnp.float32),
        ),
    )(
        first, squares, sketch, in_hbm(inverse), in_hbm(coefficients), in_hbm(weight), in_hbm(total)
    )


def split_in_three(value):
    high, _ = split(value)
    middle = value - high.astype(jnp.float32)
    middle_part = middle.astype(jnp.bfloat16)
    return high, middle_part, (middle - middle_part.astype(jnp.float32)).astype(jnp.bfloat16)


def term_kernel(
    place_ref, momentum_ref, gradient_ref, near_ref, own_ref, other_ref, term_ref, wide_ref
):
    gradient = gradient_ref[...].astype(jnp.float32)
    wide_ref[...] = gradient
    a1, a2, a3 = split_in_three(momentum_ref[...] + (gradient + near_ref[...]))
    left, right = jnp.concatenate([a1, a2], axis=1), jnp.concatenate([a1, a3], axis=1)

    def product(a, b):
        return lax.dot_general(
            a, b, (((1,), (1,)), ((), ())), preferred_element_type=jnp.float32
        )

    halves = []
    for half in range(2):
        basis = jnp.where(place_ref[0] == half, own_ref[...], other_ref[...])
        b1, b2, b3 = split_in_three(basis)
        halves.append(
            product(left, jnp.concatenate([b1, b1], axis=1))
            + (
                product(left, jnp.concatenate([b2, b2], axis=1))
                + product(right, jnp.concatenate([b3, b1], axis=1))
            )
        )
    term_ref[...] = jnp.concatenate(halves, axis=1)


def sketch_term(place, momentum, gradient, near, own, other):
    rows, columns = near.shape
    steps = 2
    step = rows // steps

    def in_half(width):
        return pl.BlockSpec((step, width), lambda i, place: (i + steps * place[1], 0))

    def by_rows(width):
        return pl.BlockSpec((step, width), lambda i, place: (i, 0))

    def whole(array):
        return pl.BlockSpec(array.shape, lambda i, place: (0, 0))

    return pl.pallas_call(
        term_kernel,
        compiler_params=pltpu.CompilerParams(vmem_limit_bytes=KERNEL_VMEM),
        grid_spec=pltpu.PrefetchScalarGridSpec(
            num_scalar_prefetch=1,
            grid=(steps,),
            in_specs=[
                in_half(columns),
                in_half(columns),
                by_rows(columns),
                whole(own),
                whole(other),
            ],
            out_specs=(by_rows(RANK), by_rows(columns)),
        ),
        out_shape=(
            jax.ShapeDtypeStruct((rows, RANK), jnp.float32),
            jax.ShapeDtypeStruct((rows, columns), jnp.float32),
        ),
    )(place, in_hbm(momentum), in_hbm(gradient), near, in_hbm(own), other)


def step(weight, momentum, right_basis, gradients):
    share = len(right_basis)
    core = jnp.reshape(lax.axis_index("fsdp"), (1,)).astype(jnp.int32)
    replica = jnp.reshape(lax.axis_index("dp"), (1,)).astype(jnp.int32)
    own = gradients[0, 0]
    half = len(own) // 2
    sent = lax.dynamic_slice_in_dim(own, (1 - lax.axis_index("dp")) * half, half, 0)
    near = swapped(sent.astype(jnp.float32), "dp")
    other_basis = swapped(right_basis, "fsdp")
    term, wide = sketch_term(
        jnp.concatenate([core, replica]), momentum, own, near, right_basis, other_basis
    )
    sketch = sum_at_owner(term, ("zl", "y", "xl"))
    wide, sketch = lax.optimization_barrier((wide, sketch))
    far = swapped(wide, "dp")
    sketch = sent_to_all(sketch, "zh").sum(axis=0)
    far, sketch = lax.optimization_barrier((far, sketch))
    sketch = gather(sketch, NEAR)

    gram, product, total = moments(replica, sketch, momentum, own, near, far)
    inverse, coefficients, squares = small_part(
        gram, swapped(gram, "fsdp"), product, swapped(product, "fsdp"), lax.axis_size(TENSOR)
    )
    squares = lax.all_to_all(squares, TENSOR, 0, 0, tiled=True)
    weight, momentum, right_basis = updates(
        core * share, squares, sketch, inverse, coefficients, weight, total, share
    )
    return weight, momentum, right_basis


def solution(mesh):
    fine = Mesh(mesh.devices.reshape(2, 2, 4, 2, 4, 2), ("dp", "fsdp", *TENSOR))
    placed = P("fsdp", TENSOR)
    return jax.shard_map(
        step,
        mesh=fine,
        in_specs=(placed, placed, placed, P(None, "dp", "fsdp", TENSOR)),
        out_specs=(placed, placed, placed),
        check_vma=False,
    )
```

```python
import math

import jax
import jax.numpy as jnp
from jax import lax
from jax.experimental import pallas as pl
from jax.experimental.pallas import tpu as pltpu
from jax.sharding import Mesh
from jax.sharding import PartitionSpec as P

D = 8192
ROWS = 4096
RANK = 256


highest = lax.Precision.HIGHEST
step_size = 0.3
drop_share = 0.05
guard_term = 1e-06

NEAR = ("dp", "zl", "y", "xl")
TENSOR = ("zh", "zl", "y", "xl")


def contract(left, right, left_dim, right_dim):
    return lax.dot_general(
        left,
        right,
        (((left_dim,), (right_dim,)), ((), ())),
        precision=highest,
        preferred_element_type=jnp.float32,
    )


def in_hbm(value):
    return pltpu.with_memory_space_constraint(value, pltpu.HBM)


def swapped(value, axis):
    return lax.ppermute(value, axis, [(0, 1), (1, 0)])


def sent_to_all(value, axis):
    length = lax.axis_size(axis)
    return lax.all_to_all(
        jnp.broadcast_to(value[None], (length, *value.shape)), axis, 0, 0, tiled=True
    )


def sum_at_owner(value, axis):
    length = lax.axis_size(axis)
    pieces = value.reshape(length, len(value) // length, *value.shape[1:])
    return lax.all_to_all(pieces, axis, 0, 0, tiled=True).sum(axis=0)


def gather(value, axis):
    pieces = sent_to_all(value, axis)
    return pieces.reshape(-1, *value.shape[1:])


KERNEL_VMEM = 16 * 2**20
BLOCK = 64
TILE = 8


def block_inverse(block):
    size = len(block)
    width = 2 * size
    rows = lax.broadcasted_iota(jnp.int32, (size, size), 0)
    columns = lax.broadcasted_iota(jnp.int32, (size, size), 1)
    both = jnp.concatenate([block, (rows == columns).astype(jnp.float32)], axis=1)
    tiles = [both[first : first + TILE] for first in range(0, size, TILE)]
    place = lax.broadcasted_iota(jnp.int32, (TILE, width), 0)

    def column(value, k):
        return jnp.broadcast_to(value[:, k : k + 1], (TILE, width))

    def row(value, k):
        return jnp.broadcast_to(value[k : k + 1, :], (TILE, width))

    def stacked(values):
        result = values[0]
        for k in range(1, TILE):
            result = jnp.where(place == k, values[k], result)
        return result

    finished = []
    for t, tile in enumerate(tiles):
        entry, factor, reciprocal, inverse = {}, {}, {}, {}
        for j in range(TILE):
            spread = column(tile, TILE * t + j)
            for i in range(j, TILE):
                entry[i, j] = row(spread, i)
        for j in range(TILE):
            reciprocal[j] = 1.0 / entry[j, j]
            for i in range(j + 1, TILE):
                factor[i, j] = entry[i, j] * reciprocal[j]
                for k in range(j + 1, i + 1):
                    entry[i, k] = entry[i, k] - factor[i, j] * entry[k, j]
        for j in range(TILE):
            for i in range(j + 1, TILE):
                total = factor[i, j]
                for k in range(j + 1, i):
                    total = total + factor[i, k] * inverse[k, j]
                inverse[i, j] = -total
        old = [row(tile, i) for i in range(TILE)]
        new = []
        for i in range(TILE):
            total = old[i]
            for j in range(i):
                total = total + inverse[i, j] * old[j]
            new.append(total)
        finished.append(stacked(new) * lax.rsqrt(stacked([entry[j, j] for j in range(TILE)])))
        for u in range(t + 1, size // TILE):
            spread = [column(tiles[u], TILE * t + j) for j in range(TILE)]
            rest = tiles[u]
            for j in range(TILE):
                total = spread[j]
                for k in range(j):
                    total = total + inverse[j, k] * spread[k]
                rest = rest - (total * reciprocal[j]) * new[j]
            tiles[u] = rest
    return jnp.concatenate(finished, axis=0)[:, size:]


def split(value):
    high = value.astype(jnp.bfloat16)
    return high, (value - high.astype(jnp.float32)).astype(jnp.bfloat16)


def three_pass(left, right, left_dim, right_dim):
    def product(a, b):
        return lax.dot_general(
            a, b, (((left_dim,), (right_dim,)), ((), ())), preferred_element_type=jnp.float32
        )

    left_high, left_low = split(left)
    right_high, right_low = split(right)
    return product(left_high, right_high) + (
        product(left_high, right_low) + product(left_low, right_high)
    )


def moments_kernel(
    replica_ref, sketch_ref, momentum_ref, own_ref, near_ref, far_ref, gram_ref, product_ref
):
    def product(a, b):
        return lax.dot_general(
            a, b, (((0,), (0,)), ((), ())), preferred_element_type=jnp.float32
        )

    half = near_ref.shape[0]
    steps = 2
    step = half // steps
    gram, one_side, moved = 0.0, 0.0, 0.0
    for part in range(2):
        for i in range(steps):
            rows = pl.ds(part * half + i * step, step)
            within = pl.ds(i * step, step)
            other = jnp.where(replica_ref[0] == part, near_ref[within, :], far_ref[within, :])
            total = momentum_ref[rows, :] + (own_ref[rows, :].astype(jnp.float32) + other)
            a1, a2, a3 = split_in_three(sketch_ref[rows, :])
            b1, b2 = split(total)
            one_side += product(a1, a2) + product(a1, a3)
            gram += product(a1, a1) + product(a2, a2)
            moved += product(a1, b1) + (product(a1, b2) + product(a2, b1))
    gram_ref[...] = gram + (one_side + one_side.T)
    product_ref[...] = moved


def moments(replica, sketch, momentum, own, near, far):
    columns = momentum.shape[1]
    return pl.pallas_call(
        moments_kernel,
        compiler_params=pltpu.CompilerParams(vmem_limit_bytes=KERNEL_VMEM),
        out_shape=(
            jax.ShapeDtypeStruct((RANK, RANK), jnp.float32),
            jax.ShapeDtypeStruct((RANK, columns), jnp.float32),
        ),
        in_specs=[pl.BlockSpec(memory_space=pltpu.SMEM)]
        + [pl.BlockSpec(memory_space=pltpu.VMEM)] * 5,
        out_specs=(pl.BlockSpec(memory_space=pltpu.VMEM),) * 2,
    )(replica, sketch, momentum, own, near, far)


def coefficients_kernel(
    gram_ref, other_gram_ref, product_ref, other_product_ref,
    inverse_ref, coefficients_ref, change_ref, squares_ref, held,
):
    held[...] = gram_ref[...] + other_gram_ref[...]
    for first in range(0, RANK, BLOCK):
        last = first + BLOCK
        inverse = block_inverse(held[first:last, first:last])
        lane = lax.broadcasted_iota(jnp.int32, (BLOCK, RANK), 1)
        row = lax.broadcasted_iota(jnp.int32, (BLOCK, RANK), 0)
        inside = (lane >= first) & (lane < last)
        panel = jnp.where(inside, (lane - first == row).astype(jnp.float32), held[first:last, :])
        panel = contract(inverse, panel, 1, 0)
        held[first:last, :] = panel
        if last < RANK:
            rest = held[last:, :]
            factor = contract(rest[:, first:last], inverse, 1, 1)
            lane = lax.broadcasted_iota(jnp.int32, (RANK - last, RANK), 1)
            inside = (lane >= first) & (lane < last)
            held[last:, :] = jnp.where(inside, 0.0, rest) - contract(factor, panel, 1, 0)
    row = lax.broadcasted_iota(jnp.int32, (RANK, RANK), 0)
    lane = lax.broadcasted_iota(jnp.int32, (RANK, RANK), 1)
    inverse = jnp.where(lane <= row, held[...], 0.0)
    coefficients = contract(inverse, product_ref[...] + other_product_ref[...], 1, 0)
    coefficients_ref[...] = coefficients
    inverse = inverse.T
    inverse_ref[...] = inverse
    change_ref[...] = drop_share * contract(inverse, coefficients, 1, 0)
    ones = jnp.ones((8, coefficients.shape[1]), jnp.float32)
    squares = contract(ones, coefficients * coefficients, 1, 1)
    squares_ref[...] = jnp.broadcast_to(squares[None, :1], squares_ref.shape)


def small_part(gram, other_gram, product, other_product, copies):
    def whole(shape):
        return pl.BlockSpec(shape, lambda i: (0,) * len(shape))

    return pl.pallas_call(
        coefficients_kernel,
        compiler_params=pltpu.CompilerParams(vmem_limit_bytes=KERNEL_VMEM),
        out_shape=(
            pltpu.HBM(gram.shape, jnp.float32),
            pltpu.HBM(product.shape, jnp.float32),
            pltpu.HBM(product.shape, jnp.float32),
            jax.ShapeDtypeStruct((copies, 1, RANK), jnp.float32),
        ),
        in_specs=[pl.BlockSpec(memory_space=pltpu.VMEM)] * 4,
        grid=(1,),
        out_specs=(
            whole(gram.shape),
            whole(product.shape),
            whole(product.shape),
            whole((copies, 1, RANK)),
        ),
        scratch_shapes=[pltpu.VMEM((RANK, RANK), jnp.float32)],
    )(gram, other_gram, product, other_product)


def momentum_kernel(
    replica_ref, sketch_ref, change_ref, momentum_ref, own_ref, near_ref, far_ref, out_ref
):
    in_own_half = pl.program_id(0) // (pl.num_programs(0) // 2) == replica_ref[0]
    other = jnp.where(in_own_half, near_ref[...], far_ref[...])
    total = momentum_ref[...] + (own_ref[...].astype(jnp.float32) + other)
    out_ref[...] = total - three_pass(sketch_ref[...], change_ref[...], 1, 0)


def new_momentum(replica, sketch, change, momentum, own, near, far):
    rows, columns = momentum.shape
    steps = 4
    step = rows // steps

    def by_rows(width):
        return pl.BlockSpec((step, width), lambda i, replica: (i, 0))

    def by_half(width):
        return pl.BlockSpec((step, width), lambda i, replica: (i % (steps // 2), 0))

    return pl.pallas_call(
        momentum_kernel,
        compiler_params=pltpu.CompilerParams(vmem_limit_bytes=KERNEL_VMEM),
        grid_spec=pltpu.PrefetchScalarGridSpec(
            num_scalar_prefetch=1,
            grid=(steps,),
            in_specs=[
                by_rows(RANK),
                pl.BlockSpec((RANK, columns), lambda i, replica: (0, 0)),
                by_rows(columns),
                by_rows(columns),
                by_half(columns),
                by_half(columns),
            ],
            out_specs=by_rows(columns),
        ),
        out_shape=jax.ShapeDtypeStruct(momentum.shape, jnp.float32),
        cost_estimate=pl.CostEstimate(
            flops=6 * rows * RANK * columns,
            bytes_accessed=4 * rows * (RANK + 2 * columns),
            transcendentals=0,
        ),
    )(replica, sketch, in_hbm(change), in_hbm(momentum), in_hbm(own), in_hbm(near), in_hbm(far))


def weight_kernel(
    first_ref, squares_ref, sketch_ref, inverse_ref, coefficients_ref, weight_ref,
    out_ref, basis_ref, near_coefficients, held, arrived, done,
):
    arrival = pltpu.make_async_copy(coefficients_ref, near_coefficients, arrived)
    arrival.start()
    step_scale = step_size * math.sqrt(ROWS * D / RANK)
    scale = lax.rsqrt(jnp.sum(squares_ref[:, 0, :], axis=0, keepdims=True) + guard_term)
    scaled = inverse_ref[...] * scale
    arrival.wait()
    change = step_scale * contract(scaled, near_coefficients[...], 1, 0)
    steps, step, _ = held.shape
    copies = []
    for i in range(steps):
        rows = pl.ds(i * step, step)
        held[i] = weight_ref[rows, :] - three_pass(sketch_ref[rows, :], change, 1, 0)
        copies.append(pltpu.make_async_copy(held.at[i], out_ref.at[rows, :], done.at[i]))
        copies[-1].start()
    share = basis_ref.shape[0]
    row = lax.broadcasted_iota(jnp.int32, (share, RANK), 0) + first_ref[0]
    lane = lax.broadcasted_iota(jnp.int32, (share, RANK), 1)
    column = jnp.sum(jnp.where(row == lane, scale, 0.0), axis=1, keepdims=True)
    first = pl.multiple_of(first_ref[0], share)
    basis_ref[...] = near_coefficients[pl.ds(first, share), :] * column
    for copy in copies:
        copy.wait()


def new_weight(first, squares, sketch, inverse, coefficients, weight, share):
    rows, columns = weight.shape
    steps = 8
    return pl.pallas_call(
        weight_kernel,
        compiler_params=pltpu.CompilerParams(vmem_limit_bytes=KERNEL_VMEM),
        out_shape=(
            jax.ShapeDtypeStruct(weight.shape, jnp.float32),
            jax.ShapeDtypeStruct((share, columns), jnp.float32),
        ),
        in_specs=[pl.BlockSpec(memory_space=pltpu.SMEM)]
        + [pl.BlockSpec(memory_space=pltpu.VMEM)] * 3
        + [pl.BlockSpec(memory_space=pl.ANY), pl.BlockSpec(memory_space=pltpu.VMEM)],
        out_specs=(
            pl.BlockSpec(memory_space=pl.ANY),
            pl.BlockSpec(memory_space=pltpu.VMEM),
        ),
        scratch_shapes=[
            pltpu.VMEM(coefficients.shape, jnp.float32),
            pltpu.VMEM((steps, rows // steps, columns), jnp.float32),
            pltpu.SemaphoreType.DMA,
            pltpu.SemaphoreType.DMA((steps,)),
        ],
    )(first, squares, sketch, inverse, in_hbm(coefficients), weight)


def split_in_three(value):
    high, _ = split(value)
    middle = value - high.astype(jnp.float32)
    middle_part = middle.astype(jnp.bfloat16)
    return high, middle_part, (middle - middle_part.astype(jnp.float32)).astype(jnp.bfloat16)


def spread_basis(core, own, other, half):
    return split_in_three(jnp.where(core == half, own, other))


def pair(a, b):
    return jnp.concatenate([a, b], axis=1)


def row_product(a, b):
    return lax.dot_general(a, b, (((1,), (1,)), ((), ())), preferred_element_type=jnp.float32)


def first_term_kernel(place_ref, momentum_ref, gradient_ref, own_ref, other_ref, term_ref, wide_ref):
    gradient = gradient_ref[...].astype(jnp.float32)
    wide_ref[...] = gradient
    a1, a2, a3 = split_in_three(momentum_ref[...] + gradient)
    left, right = pair(a1, a2), pair(a1, a3)
    for half in range(2):
        b1, b2, b3 = spread_basis(place_ref[0], own_ref[...], other_ref[...], half)
        share = own_ref.shape[0]
        term_ref[:, half * share : half * share + share] = row_product(left, pair(b1, b1)) + (
            row_product(left, pair(b2, b2)) + row_product(right, pair(b3, b1))
        )


def second_term_kernel(place_ref, near_ref, first_ref, own_ref, other_ref, term_ref):
    near = near_ref[...].astype(jnp.bfloat16)
    twice = pair(near, near)
    for half in range(2):
        b1, b2, b3 = spread_basis(place_ref[0], own_ref[...], other_ref[...], half)
        share = own_ref.shape[0]
        columns = slice(half * share, half * share + share)
        term_ref[:, columns] = first_ref[:, columns] + (
            row_product(twice, pair(b1, b2)) + row_product(near, b3)
        )


def first_term(place, momentum, gradient, own, other):
    rows, columns = len(momentum) // 2, momentum.shape[1]
    steps = 2
    step = rows // steps

    def in_half(width):
        return pl.BlockSpec((step, width), lambda i, place: (i + steps * place[1], 0))

    def by_rows(width):
        return pl.BlockSpec((step, width), lambda i, place: (i, 0))

    def whole(array):
        return pl.BlockSpec(array.shape, lambda i, place: (0, 0))

    return pl.pallas_call(
        first_term_kernel,
        compiler_params=pltpu.CompilerParams(vmem_limit_bytes=KERNEL_VMEM),
        grid_spec=pltpu.PrefetchScalarGridSpec(
            num_scalar_prefetch=1,
            grid=(steps,),
            in_specs=[in_half(columns), in_half(columns), whole(own), whole(other)],
            out_specs=(by_rows(RANK), by_rows(columns)),
        ),
        out_shape=(
            jax.ShapeDtypeStruct((rows, RANK), jnp.float32),
            jax.ShapeDtypeStruct((rows, columns), jnp.float32),
        ),
        cost_estimate=pl.CostEstimate(
            flops=12 * rows * RANK * columns,
            bytes_accessed=4 * rows * (RANK + 3 * columns),
            transcendentals=0,
        ),
    )(place, in_hbm(momentum), in_hbm(gradient), in_hbm(own), other)


def second_term(place, near, first, own, other):
    return pl.pallas_call(
        second_term_kernel,
        compiler_params=pltpu.CompilerParams(vmem_limit_bytes=KERNEL_VMEM),
        out_shape=jax.ShapeDtypeStruct(first.shape, jnp.float32),
        in_specs=[pl.BlockSpec(memory_space=pltpu.SMEM)]
        + [pl.BlockSpec(memory_space=pltpu.VMEM)] * 4,
        out_specs=pl.BlockSpec(memory_space=pltpu.VMEM),
    )(place, near, first, own, other)


def step(weight, momentum, right_basis, gradients):
    share = len(right_basis)
    core = jnp.reshape(lax.axis_index("fsdp"), (1,)).astype(jnp.int32)
    replica = jnp.reshape(lax.axis_index("dp"), (1,)).astype(jnp.int32)
    own = gradients[0, 0]
    half = len(own) // 2
    sent = lax.dynamic_slice_in_dim(own, (1 - lax.axis_index("dp")) * half, half, 0)
    near = swapped(sent.astype(jnp.float32), "dp")
    other_basis = swapped(right_basis, "fsdp")
    place = jnp.concatenate([core, replica])
    term, wide = first_term(place, momentum, own, right_basis, other_basis)
    term = second_term(place, near, term, right_basis, other_basis)
    sketch = sum_at_owner(term, ("zl", "y", "xl"))
    wide, sketch = lax.optimization_barrier((wide, sketch))
    far = swapped(wide, "dp")
    sketch = sketch + lax.ppermute(sketch, "zh", [(0, 1), (1, 0), (2, 3), (3, 2)])
    sketch = sketch + lax.ppermute(sketch, "zh", [(0, 3), (3, 0), (1, 2), (2, 1)])
    far, sketch = lax.optimization_barrier((far, sketch))
    sketch = gather(sketch, NEAR)

    gram, product = moments(replica, sketch, momentum, own, near, far)
    inverse, coefficients, change, squares = small_part(
        gram, swapped(gram, "fsdp"), product, swapped(product, "fsdp"), lax.axis_size(TENSOR)
    )
    squares = lax.all_to_all(squares, TENSOR, 0, 0, tiled=True)
    momentum = new_momentum(replica, sketch, change, momentum, own, near, far)
    weight, right_basis = new_weight(
        core * share, squares, sketch, inverse, coefficients, weight, share
    )
    return weight, momentum, right_basis


def solution(mesh):
    fine = Mesh(mesh.devices.reshape(2, 2, 4, 2, 4, 2), ("dp", "fsdp", *TENSOR))
    placed = P("fsdp", TENSOR)
    return jax.shard_map(
        step,
        mesh=fine,
        in_specs=(placed, placed, placed, P(None, "dp", "fsdp", TENSOR)),
        out_specs=(placed, placed, placed),
        check_vma=False,
    )
```

```python
import math

import jax
import jax.numpy as jnp
from jax import lax
from jax.experimental import pallas as pl
from jax.experimental.pallas import tpu as pltpu
from jax.sharding import Mesh
from jax.sharding import PartitionSpec as P

D = 8192
ROWS = 4096
RANK = 256


highest = lax.Precision.HIGHEST
step_size = 0.3
drop_share = 0.05
guard_term = 1e-06

NEAR = ("dp", "zl", "y", "xl")
TENSOR = ("zh", "zl", "y", "xl")


def contract(left, right, left_dim, right_dim):
    return lax.dot_general(
        left,
        right,
        (((left_dim,), (right_dim,)), ((), ())),
        precision=highest,
        preferred_element_type=jnp.float32,
    )


def in_hbm(value):
    return pltpu.with_memory_space_constraint(value, pltpu.HBM)


def swapped(value, axis):
    return lax.ppermute(value, axis, [(0, 1), (1, 0)])


def sent_to_all(value, axis):
    length = lax.axis_size(axis)
    return lax.all_to_all(
        jnp.broadcast_to(value[None], (length, *value.shape)), axis, 0, 0, tiled=True
    )


def sum_at_owner(value, axis):
    length = lax.axis_size(axis)
    pieces = value.reshape(length, len(value) // length, *value.shape[1:])
    return lax.all_to_all(pieces, axis, 0, 0, tiled=True).sum(axis=0)


def gather(value, axis):
    pieces = sent_to_all(value, axis)
    return pieces.reshape(-1, *value.shape[1:])


KERNEL_VMEM = 16 * 2**20
BLOCK = 64
TILE = 8


def block_inverse(block):
    size = len(block)
    width = 2 * size
    rows = lax.broadcasted_iota(jnp.int32, (size, size), 0)
    columns = lax.broadcasted_iota(jnp.int32, (size, size), 1)
    both = jnp.concatenate([block, (rows == columns).astype(jnp.float32)], axis=1)
    tiles = [both[first : first + TILE] for first in range(0, size, TILE)]
    place = lax.broadcasted_iota(jnp.int32, (TILE, width), 0)

    def column(value, k):
        return jnp.broadcast_to(value[:, k : k + 1], (TILE, width))

    def row(value, k):
        return jnp.broadcast_to(value[k : k + 1, :], (TILE, width))

    def stacked(values):
        result = values[0]
        for k in range(1, TILE):
            result = jnp.where(place == k, values[k], result)
        return result

    finished = []
    for t, tile in enumerate(tiles):
        entry, factor, reciprocal, inverse = {}, {}, {}, {}
        for j in range(TILE):
            spread = column(tile, TILE * t + j)
            for i in range(j, TILE):
                entry[i, j] = row(spread, i)
        for j in range(TILE):
            reciprocal[j] = 1.0 / entry[j, j]
            for i in range(j + 1, TILE):
                factor[i, j] = entry[i, j] * reciprocal[j]
                for k in range(j + 1, i + 1):
                    entry[i, k] = entry[i, k] - factor[i, j] * entry[k, j]
        for j in range(TILE):
            for i in range(j + 1, TILE):
                total = factor[i, j]
                for k in range(j + 1, i):
                    total = total + factor[i, k] * inverse[k, j]
                inverse[i, j] = -total
        old = [row(tile, i) for i in range(TILE)]
        new = []
        for i in range(TILE):
            total = old[i]
            for j in range(i):
                total = total + inverse[i, j] * old[j]
            new.append(total)
        finished.append(stacked(new) * lax.rsqrt(stacked([entry[j, j] for j in range(TILE)])))
        for u in range(t + 1, size // TILE):
            spread = [column(tiles[u], TILE * t + j) for j in range(TILE)]
            rest = tiles[u]
            for j in range(TILE):
                total = spread[j]
                for k in range(j):
                    total = total + inverse[j, k] * spread[k]
                rest = rest - (total * reciprocal[j]) * new[j]
            tiles[u] = rest
    return jnp.concatenate(finished, axis=0)[:, size:]


def split(value):
    high = value.astype(jnp.bfloat16)
    return high, (value - high.astype(jnp.float32)).astype(jnp.bfloat16)


def three_pass(left, right, left_dim, right_dim):
    def product(a, b):
        return lax.dot_general(
            a, b, (((left_dim,), (right_dim,)), ((), ())), preferred_element_type=jnp.float32
        )

    left_high, left_low = split(left)
    right_high, right_low = split(right)
    width = right.shape[1]
    high = product(left_high, jnp.concatenate([right_high, right_low], axis=1))
    return high[:, :width] + (high[:, width:] + product(left_low, right_high))


def moments_kernel(
    replica_ref, sketch_ref, momentum_ref, own_ref, near_ref, far_ref, gram_ref, product_ref
):
    def product(a, b):
        return lax.dot_general(
            a, b, (((0,), (0,)), ((), ())), preferred_element_type=jnp.float32
        )

    half = near_ref.shape[0]
    steps = 2
    step = half // steps
    gram, one_side, moved = 0.0, 0.0, 0.0
    for part in range(2):
        for i in range(steps):
            rows = pl.ds(part * half + i * step, step)
            within = pl.ds(i * step, step)
            other = jnp.where(replica_ref[0] == part, near_ref[within, :], far_ref[within, :])
            total = momentum_ref[rows, :] + (own_ref[rows, :].astype(jnp.float32) + other)
            a1, a2, a3 = split_in_three(sketch_ref[rows, :])
            b1, b2 = split(total)
            one_side += product(a1, a2) + product(a1, a3)
            gram += product(a1, a1) + product(a2, a2)
            high = product(a1, jnp.concatenate([b1, b2], axis=1))
            width = b1.shape[1]
            moved += high[:, :width] + (high[:, width:] + product(a2, b1))
    gram_ref[...] = gram + (one_side + one_side.T)
    product_ref[...] = moved


def moments(replica, sketch, momentum, own, near, far):
    columns = momentum.shape[1]
    return pl.pallas_call(
        moments_kernel,
        compiler_params=pltpu.CompilerParams(vmem_limit_bytes=KERNEL_VMEM),
        out_shape=(
            jax.ShapeDtypeStruct((RANK, RANK), jnp.float32),
            jax.ShapeDtypeStruct((RANK, columns), jnp.float32),
        ),
        in_specs=[pl.BlockSpec(memory_space=pltpu.SMEM)]
        + [pl.BlockSpec(memory_space=pltpu.VMEM)] * 5,
        out_specs=(pl.BlockSpec(memory_space=pltpu.VMEM),) * 2,
    )(replica, sketch, momentum, own, near, far)


def coefficients_kernel(
    gram_ref, other_gram_ref, product_ref, other_product_ref,
    inverse_ref, coefficients_ref, change_ref, squares_ref, held,
):
    held[...] = gram_ref[...] + other_gram_ref[...]
    for first in range(0, RANK, BLOCK):
        last = first + BLOCK
        inverse = block_inverse(held[first:last, first:last])
        lane = lax.broadcasted_iota(jnp.int32, (BLOCK, RANK), 1)
        row = lax.broadcasted_iota(jnp.int32, (BLOCK, RANK), 0)
        inside = (lane >= first) & (lane < last)
        panel = jnp.where(inside, (lane - first == row).astype(jnp.float32), held[first:last, :])
        panel = contract(inverse, panel, 1, 0)
        held[first:last, :] = panel
        if last < RANK:
            rest = held[last:, :]
            factor = contract(rest[:, first:last], inverse, 1, 1)
            lane = lax.broadcasted_iota(jnp.int32, (RANK - last, RANK), 1)
            inside = (lane >= first) & (lane < last)
            held[last:, :] = jnp.where(inside, 0.0, rest) - contract(factor, panel, 1, 0)
    row = lax.broadcasted_iota(jnp.int32, (RANK, RANK), 0)
    lane = lax.broadcasted_iota(jnp.int32, (RANK, RANK), 1)
    inverse = jnp.where(lane <= row, held[...], 0.0)
    coefficients = contract(inverse, product_ref[...] + other_product_ref[...], 1, 0)
    coefficients_ref[...] = coefficients
    inverse = inverse.T
    inverse_ref[...] = inverse
    change_ref[...] = drop_share * contract(inverse, coefficients, 1, 0)
    ones = jnp.ones((8, coefficients.shape[1]), jnp.float32)
    squares = contract(ones, coefficients * coefficients, 1, 1)
    squares_ref[...] = jnp.broadcast_to(squares[None, :1], squares_ref.shape)


def small_part(gram, other_gram, product, other_product, copies):
    def whole(shape):
        return pl.BlockSpec(shape, lambda i: (0,) * len(shape))

    return pl.pallas_call(
        coefficients_kernel,
        compiler_params=pltpu.CompilerParams(vmem_limit_bytes=KERNEL_VMEM),
        out_shape=(
            pltpu.HBM(gram.shape, jnp.float32),
            pltpu.HBM(product.shape, jnp.float32),
            pltpu.HBM(product.shape, jnp.float32),
            jax.ShapeDtypeStruct((copies, 1, RANK), jnp.float32),
        ),
        in_specs=[pl.BlockSpec(memory_space=pltpu.VMEM)] * 4,
        grid=(1,),
        out_specs=(
            whole(gram.shape),
            whole(product.shape),
            whole(product.shape),
            whole((copies, 1, RANK)),
        ),
        scratch_shapes=[pltpu.VMEM((RANK, RANK), jnp.float32)],
    )(gram, other_gram, product, other_product)


def momentum_kernel(
    replica_ref, sketch_ref, change_ref, momentum_ref, own_ref, near_ref, far_ref, out_ref
):
    in_own_half = pl.program_id(0) // (pl.num_programs(0) // 2) == replica_ref[0]
    other = jnp.where(in_own_half, near_ref[...], far_ref[...])
    total = momentum_ref[...] + (own_ref[...].astype(jnp.float32) + other)
    out_ref[...] = total - three_pass(sketch_ref[...], change_ref[...], 1, 0)


def new_momentum(replica, sketch, change, momentum, own, near, far):
    rows, columns = momentum.shape
    steps = 4
    step = rows // steps

    def by_rows(width):
        return pl.BlockSpec((step, width), lambda i, replica: (i, 0))

    def by_half(width):
        return pl.BlockSpec((step, width), lambda i, replica: (i % (steps // 2), 0))

    return pl.pallas_call(
        momentum_kernel,
        compiler_params=pltpu.CompilerParams(vmem_limit_bytes=KERNEL_VMEM),
        grid_spec=pltpu.PrefetchScalarGridSpec(
            num_scalar_prefetch=1,
            grid=(steps,),
            in_specs=[
                by_rows(RANK),
                pl.BlockSpec((RANK, columns), lambda i, replica: (0, 0)),
                by_rows(columns),
                by_rows(columns),
                by_half(columns),
                by_half(columns),
            ],
            out_specs=by_rows(columns),
        ),
        out_shape=jax.ShapeDtypeStruct(momentum.shape, jnp.float32),
        cost_estimate=pl.CostEstimate(
            flops=6 * rows * RANK * columns,
            bytes_accessed=4 * rows * (RANK + 2 * columns),
            transcendentals=0,
        ),
    )(replica, sketch, in_hbm(change), in_hbm(momentum), in_hbm(own), in_hbm(near), in_hbm(far))


def weight_kernel(
    first_ref, squares_ref, sketch_ref, inverse_ref, coefficients_ref, weight_ref,
    out_ref, basis_ref, near_coefficients, held, arrived, done,
):
    arrival = pltpu.make_async_copy(coefficients_ref, near_coefficients, arrived)
    arrival.start()
    step_scale = step_size * math.sqrt(ROWS * D / RANK)
    scale = lax.rsqrt(jnp.sum(squares_ref[:, 0, :], axis=0, keepdims=True) + guard_term)
    scaled = inverse_ref[...] * scale
    arrival.wait()
    change = step_scale * contract(scaled, near_coefficients[...], 1, 0)
    steps, step, _ = held.shape
    copies = []
    for i in range(steps):
        rows = pl.ds(i * step, step)
        held[i] = weight_ref[rows, :] - three_pass(sketch_ref[rows, :], change, 1, 0)
        copies.append(pltpu.make_async_copy(held.at[i], out_ref.at[rows, :], done.at[i]))
        copies[-1].start()
    share = basis_ref.shape[0]
    row = lax.broadcasted_iota(jnp.int32, (share, RANK), 0) + first_ref[0]
    lane = lax.broadcasted_iota(jnp.int32, (share, RANK), 1)
    column = jnp.sum(jnp.where(row == lane, scale, 0.0), axis=1, keepdims=True)
    first = pl.multiple_of(first_ref[0], share)
    basis_ref[...] = near_coefficients[pl.ds(first, share), :] * column
    for copy in copies:
        copy.wait()


def new_weight(first, squares, sketch, inverse, coefficients, weight, share):
    rows, columns = weight.shape
    steps = 4
    return pl.pallas_call(
        weight_kernel,
        compiler_params=pltpu.CompilerParams(vmem_limit_bytes=KERNEL_VMEM),
        out_shape=(
            jax.ShapeDtypeStruct(weight.shape, jnp.float32),
            jax.ShapeDtypeStruct((share, columns), jnp.float32),
        ),
        in_specs=[pl.BlockSpec(memory_space=pltpu.SMEM)]
        + [pl.BlockSpec(memory_space=pltpu.VMEM)] * 3
        + [pl.BlockSpec(memory_space=pl.ANY), pl.BlockSpec(memory_space=pltpu.VMEM)],
        out_specs=(
            pl.BlockSpec(memory_space=pl.ANY),
            pl.BlockSpec(memory_space=pltpu.VMEM),
        ),
        scratch_shapes=[
            pltpu.VMEM(coefficients.shape, jnp.float32),
            pltpu.VMEM((steps, rows // steps, columns), jnp.float32),
            pltpu.SemaphoreType.DMA,
            pltpu.SemaphoreType.DMA((steps,)),
        ],
    )(first, squares, sketch, inverse, in_hbm(coefficients), weight)


def split_in_three(value):
    high, _ = split(value)
    middle = value - high.astype(jnp.float32)
    middle_part = middle.astype(jnp.bfloat16)
    return high, middle_part, (middle - middle_part.astype(jnp.float32)).astype(jnp.bfloat16)


def spread_basis(core, own, other, half):
    return split_in_three(jnp.where(core == half, own, other))


def pair(a, b):
    return jnp.concatenate([a, b], axis=1)


def row_product(a, b):
    return lax.dot_general(a, b, (((1,), (1,)), ((), ())), preferred_element_type=jnp.float32)


def first_term_kernel(place_ref, momentum_ref, gradient_ref, own_ref, other_ref, term_ref, wide_ref):
    gradient = gradient_ref[...].astype(jnp.float32)
    wide_ref[...] = gradient
    a1, a2, a3 = split_in_three(momentum_ref[...] + gradient)
    left, right = pair(a1, a2), pair(a1, a3)
    for half in range(2):
        b1, b2, b3 = spread_basis(place_ref[0], own_ref[...], other_ref[...], half)
        share = own_ref.shape[0]
        term_ref[:, half * share : half * share + share] = row_product(left, pair(b1, b1)) + (
            row_product(left, pair(b2, b2)) + row_product(right, pair(b3, b1))
        )


def second_term_kernel(place_ref, near_ref, first_ref, own_ref, other_ref, term_ref):
    near = near_ref[...].astype(jnp.bfloat16)
    twice = pair(near, near)
    for half in range(2):
        b1, b2, b3 = spread_basis(place_ref[0], own_ref[...], other_ref[...], half)
        share = own_ref.shape[0]
        columns = slice(half * share, half * share + share)
        term_ref[:, columns] = first_ref[:, columns] + (
            row_product(twice, pair(b1, b2)) + row_product(near, b3)
        )


def first_term(place, momentum, gradient, own, other):
    rows, columns = len(momentum) // 2, momentum.shape[1]
    steps = 2
    step = rows // steps

    def in_half(width):
        return pl.BlockSpec((step, width), lambda i, place: (i + steps * place[1], 0))

    def by_rows(width):
        return pl.BlockSpec((step, width), lambda i, place: (i, 0))

    def whole(array):
        return pl.BlockSpec(array.shape, lambda i, place: (0, 0))

    return pl.pallas_call(
        first_term_kernel,
        compiler_params=pltpu.CompilerParams(vmem_limit_bytes=KERNEL_VMEM),
        grid_spec=pltpu.PrefetchScalarGridSpec(
            num_scalar_prefetch=1,
            grid=(steps,),
            in_specs=[in_half(columns), in_half(columns), whole(own), whole(other)],
            out_specs=(by_rows(RANK), by_rows(columns)),
        ),
        out_shape=(
            jax.ShapeDtypeStruct((rows, RANK), jnp.float32),
            jax.ShapeDtypeStruct((rows, columns), jnp.float32),
        ),
        cost_estimate=pl.CostEstimate(
            flops=12 * rows * RANK * columns,
            bytes_accessed=4 * rows * (RANK + 3 * columns),
            transcendentals=0,
        ),
    )(place, in_hbm(momentum), in_hbm(gradient), in_hbm(own), other)


def second_term(place, near, first, own, other):
    return pl.pallas_call(
        second_term_kernel,
        compiler_params=pltpu.CompilerParams(vmem_limit_bytes=KERNEL_VMEM),
        out_shape=jax.ShapeDtypeStruct(first.shape, jnp.float32),
        in_specs=[pl.BlockSpec(memory_space=pltpu.SMEM)]
        + [pl.BlockSpec(memory_space=pltpu.VMEM)] * 4,
        out_specs=pl.BlockSpec(memory_space=pltpu.VMEM),
    )(place, near, first, own, other)


def step(weight, momentum, right_basis, gradients):
    share = len(right_basis)
    core = jnp.reshape(lax.axis_index("fsdp"), (1,)).astype(jnp.int32)
    replica = jnp.reshape(lax.axis_index("dp"), (1,)).astype(jnp.int32)
    own = gradients[0, 0]
    half = len(own) // 2
    sent = lax.dynamic_slice_in_dim(own, (1 - lax.axis_index("dp")) * half, half, 0)
    near = swapped(sent.astype(jnp.float32), "dp")
    other_basis = swapped(right_basis, "fsdp")
    place = jnp.concatenate([core, replica])
    term, wide = first_term(place, momentum, own, right_basis, other_basis)
    term = second_term(place, near, term, right_basis, other_basis)
    sketch = sum_at_owner(term, ("zl", "y", "xl"))
    wide, sketch = lax.optimization_barrier((wide, sketch))
    far = swapped(wide, "dp")
    sketch = sketch + lax.ppermute(sketch, "zh", [(0, 1), (1, 0), (2, 3), (3, 2)])
    sketch = sketch + lax.ppermute(sketch, "zh", [(0, 3), (3, 0), (1, 2), (2, 1)])
    far, sketch = lax.optimization_barrier((far, sketch))
    sketch = gather(sketch, NEAR)

    gram, product = moments(replica, sketch, momentum, own, near, far)
    inverse, coefficients, change, squares = small_part(
        gram, swapped(gram, "fsdp"), product, swapped(product, "fsdp"), lax.axis_size(TENSOR)
    )
    squares = lax.all_to_all(squares, TENSOR, 0, 0, tiled=True)
    momentum = new_momentum(replica, sketch, change, momentum, own, near, far)
    weight, right_basis = new_weight(
        core * share, squares, sketch, inverse, coefficients, weight, share
    )
    return weight, momentum, right_basis


def solution(mesh):
    fine = Mesh(mesh.devices.reshape(2, 2, 4, 2, 4, 2), ("dp", "fsdp", *TENSOR))
    placed = P("fsdp", TENSOR)
    return jax.shard_map(
        step,
        mesh=fine,
        in_specs=(placed, placed, placed, P(None, "dp", "fsdp", TENSOR)),
        out_specs=(placed, placed, placed),
        check_vma=False,
    )
```
